32 devices in a mesh: rep: 8 (over z, y), grp: 4 (over x, core).
Axes of the slice: x: 2, y: 2, z: 4, core: 2. Of those that a mesh axis runs over, the one named last changes fastest.
Arguments:
- block_input: bfloat16 [8, 768, 1152], P('rep', 'grp'), may hold values from -6 to 6
- lengths: int32 [8], P('rep'), may hold values from 384 to 768, as said below
- ln1_gain: bfloat16 [1152], P('grp'), may hold values from 0.5 to 1.5
- ln1_bias: bfloat16 [1152], P('grp'), may hold values from -3 to 3
- w_qkv: bfloat16 [1152, 3456], P('grp'), as said below
- b_qv: bfloat16 [2304], P('grp'), may hold values from -3 to 3
- w_out: bfloat16 [1152, 1152], P('grp'), may hold values from -3.5 to 3.5
- b_out: bfloat16 [1152], P('grp'), may hold values from -3 to 3
- ln2_gain: bfloat16 [1152], P('grp'), may hold values from 0.5 to 1.5
- ln2_bias: bfloat16 [1152], P('grp'), may hold values from -3 to 3
- w_up: bfloat16 [1152, 4304], P(None, 'grp'), may hold values from -0.1875 to 0.1875
- b_up: bfloat16 [4304], P('grp'), may hold values from -3 to 3
- w_down: bfloat16 [4304, 1152], P('grp'), may hold values from -0.09375 to 0.09375
- b_down: bfloat16 [1152], P('grp'), may hold values from -3 to 3
- cotangent: bfloat16 [8, 768, 1152], P('rep', 'grp'), may hold values from -6 to 6
Outputs:
- block_output: bfloat16 [8, 768, 1152], P('rep', 'grp')
- grad_input: bfloat16 [8, 768, 1152], P('rep', 'grp')
- grad_ln1_gain: float32 [1152], P('grp')
- grad_ln1_bias: float32 [1152], P('grp')
- grad_w_qkv: float32 [1152, 3456], P('grp', 'rep')
- grad_b_qv: float32 [2304], P('grp')
- grad_w_out: float32 [1152, 1152], P('grp', 'rep')
- grad_b_out: float32 [1152], P('grp')
- grad_ln2_gain: float32 [1152], P('grp')
- grad_ln2_bias: float32 [1152], P('grp')
- grad_w_up: float32 [1152, 4304], P('rep', 'grp')
- grad_b_up: float32 [4304], P('grp')
- grad_w_down: float32 [4304, 1152], P('grp', 'rep')
- grad_b_down: float32 [1152], P('grp')
The draws below stay inside these ranges and needn't reach their ends.
Inputs may be any that keep to these rules, and one draw needn't show every extreme that they name: `lengths`: valid tokens of each image, counted from its first slot. `w_qkv`: query, key and value projections in this column order.
All inputs are finite; a program needn't handle non-finite values.
Results may differ from the reference program's by a relative error of at most 0.012.
Values may be sent and summed in bfloat16 or wider, within the bound.
No kernel may reach another device: no remote copies, remote signals or barrier semaphores. Data moves between devices by JAX's collectives and lax.ppermute only.
A program may use at most 192 MiB of HBM per device.

```python
import math
import jax
import jax.numpy as jnp
from jax import lax

D = 1152
HEADS = 16
MLP = 4304
SEQ = 768
IMAGES = 8


def draw_lengths(key, part):
    first_key, second_key, third_key = jax.random.split(key, 3)
    counts = jax.random.randint(first_key, (IMAGES,), SEQ // 2, SEQ + 1)
    longest = jax.random.randint(second_key, (), 0, IMAGES)
    shortest = (longest + jax.random.randint(third_key, (), 1, IMAGES)) % IMAGES
    counts = counts.at[longest].set(SEQ).at[shortest].set(SEQ // 2)
    return counts.astype(jnp.int32)


def draw_w_qkv(key, part):
    base_key = jax.random.fold_in(key, 0)
    base = jax.random.normal(base_key, (D, 3 * D), jnp.float32) / math.sqrt(D)
    return base.astype(jnp.bfloat16)


def shard_levels(key, dims, cuts, least, top_value):
    loudness = 1.0
    for dim, parts in cuts:
        draws = jax.random.uniform(jax.random.fold_in(jax.random.fold_in(key, 6), dim), (parts,), jnp.float32, least / len(cuts), top_value / len(cuts))
        loudness = loudness * jnp.repeat(jnp.exp(draws), dims[dim] // parts).reshape((-1,) + (1,) * (len(dims) - 1 - dim))
    return loudness


def bell_draw(rng, shape, deviation, reach, cuts=(), kind=jnp.bfloat16):
    level = shard_levels(rng, shape, cuts, -0.22, 0.18) if cuts else 1.0
    array = jax.random.normal(rng, shape, jnp.float32) * deviation * level
    return jnp.minimum(jnp.maximum(array, -reach), reach).astype(kind)


def setup_inputs(seed: int = 0) -> dict:
    arg_keys = jax.random.split(jax.random.key(seed), 16)
    block_input = bell_draw(arg_keys[0], (IMAGES, SEQ, D), 1.0, 6.0, ((0, 8), (1, 4)))
    lengths = draw_lengths(jax.random.fold_in(arg_keys[15], 71), 0)
    ln1_gain = jnp.clip(1.0 + 0.1 * jax.random.normal(arg_keys[2], (D,), jnp.float32), 0.5, 1.5).astype(jnp.bfloat16)
    ln1_bias = bell_draw(arg_keys[3], (D,), 0.5, 3.0, ((0, 4),))
    w_qkv = draw_w_qkv(jax.random.fold_in(arg_keys[15], 71), 0)
    b_qv = bell_draw(arg_keys[5], (2 * D,), 0.5, 3.0, ((0, 4),))
    w_out = bell_draw(arg_keys[6], (D, D), (max(2 * D // SEQ, 1)) ** -0.5, 3.5, ((0, 4),))
    b_out = bell_draw(arg_keys[7], (D,), 0.5, 3.0, ((0, 4),))
    ln2_gain = jnp.clip(1.0 + 0.1 * jax.random.normal(arg_keys[8], (D,), jnp.float32), 0.5, 1.5).astype(jnp.bfloat16)
    ln2_bias = bell_draw(arg_keys[9], (D,), 0.5, 3.0, ((0, 4),))
    w_up = bell_draw(arg_keys[10], (D, MLP), D ** -0.5, 0.1875, ((1, 4),))
    b_up = bell_draw(arg_keys[11], (MLP,), 0.5, 3.0, ((0, 4),))
    w_down = bell_draw(arg_keys[12], (MLP, D), MLP ** -0.5, 0.09375, ((0, 4),))
    b_down = bell_draw(arg_keys[13], (D,), 0.5, 3.0, ((0, 4),))
    cotangent = bell_draw(arg_keys[14], (IMAGES, SEQ, D), 1.0, 6.0, ((0, 8), (1, 4)))
    return dict(block_input=block_input, lengths=lengths, ln1_gain=ln1_gain, ln1_bias=ln1_bias, w_qkv=w_qkv, b_qv=b_qv, w_out=w_out, b_out=b_out, ln2_gain=ln2_gain, ln2_bias=ln2_bias, w_up=w_up, b_up=b_up, w_down=w_down, b_down=b_down, cotangent=cotangent)


EPSILON = 1e-06
GELU_SCALE = 0.7978845608028654
GELU_CUBIC = 0.044715
NEG_FILL = -1000000000.0

def layer_norm(values, gain, shift):
    center = values - lax.optimization_barrier(jnp.mean(values, axis=-1, keepdims=True))
    inv_std = lax.rsqrt(lax.optimization_barrier(jnp.mean(center * center, axis=-1, keepdims=True)) + EPSILON)
    normed = center * inv_std
    return (normed * gain + shift, normed, inv_std)

def norm_backward(upstream, normed, inv_std, gain):
    scaled = upstream * gain
    return inv_std * (scaled - lax.optimization_barrier(jnp.mean(scaled, axis=-1, keepdims=True)) - normed * lax.optimization_barrier(jnp.mean(scaled * normed, axis=-1, keepdims=True)))

def gelu_with_slope(values):
    cubic = values * values * values
    tangent = jnp.tanh(GELU_SCALE * (values + GELU_CUBIC * cubic))
    output = 0.5 * values * (1.0 + tangent)
    slope = 0.5 * (1.0 + tangent) + 0.5 * values * (1.0 - tangent * tangent) * GELU_SCALE * (1.0 + 3.0 * GELU_CUBIC * values * values)
    return (output, slope)

def split_heads(rows):
    return rows.astype(jnp.float32).reshape(rows.shape[0], HEADS, rows.shape[1] // HEADS)

def image_pass(image_in, valid_count, upstream, params):
    ln1_gain, ln1_bias, w_qkv, b_qv, w_out, b_out, ln2_gain, ln2_bias, w_up, b_up, w_down, b_down = params
    seq_len = image_in.shape[0]
    model_width = image_in.shape[1]
    score_scale = 1.0 / math.sqrt(model_width // HEADS)
    residual_in = image_in.astype(jnp.float32)
    normed_out, normed_one, inv_one = layer_norm(residual_in, ln1_gain.astype(jnp.float32), ln1_bias.astype(jnp.float32))
    first_input = normed_out.astype(jnp.bfloat16)
    projected = jnp.dot(first_input, w_qkv, preferred_element_type=jnp.float32)
    bias_wide = b_qv.astype(jnp.float32)
    queries = (projected[:, :model_width] + bias_wide[:model_width]).astype(jnp.bfloat16)
    key_rows = projected[:, model_width:2 * model_width].astype(jnp.bfloat16)
    value_rows = (projected[:, 2 * model_width:] + bias_wide[model_width:]).astype(jnp.bfloat16)
    live = jnp.arange(seq_len) < valid_count
    query_heads = split_heads(queries)
    key_heads = split_heads(key_rows)
    value_heads = split_heads(value_rows)
    scores = jnp.einsum('qhd,khd->hqk', query_heads, key_heads) * score_scale
    scores = jnp.where(live[None, None, :], scores, NEG_FILL)
    top = lax.optimization_barrier(jnp.max(scores, axis=-1, keepdims=True))
    log_total = top + jnp.log(lax.optimization_barrier(jnp.sum(jnp.exp(scores - top), axis=-1, keepdims=True)))
    probs_wide = jnp.exp(scores - log_total)
    probs = probs_wide.astype(jnp.bfloat16)
    mixed = jnp.einsum('hqk,khd->qhd', probs.astype(jnp.float32), value_heads)
    mixed = mixed.reshape(seq_len, model_width).astype(jnp.bfloat16)
    residual_mid = residual_in + (jnp.dot(mixed, w_out, preferred_element_type=jnp.float32) + b_out.astype(jnp.float32))
    normed_out2, normed_two, inv_two = layer_norm(residual_mid, ln2_gain.astype(jnp.float32), ln2_bias.astype(jnp.float32))
    second_input = normed_out2.astype(jnp.bfloat16)
    pre_act = jnp.dot(second_input, w_up, preferred_element_type=jnp.float32) + b_up.astype(jnp.float32)
    activated_wide, slope = gelu_with_slope(pre_act)
    activated = activated_wide.astype(jnp.bfloat16)
    block_rows = residual_mid + (jnp.dot(activated, w_down, preferred_element_type=jnp.float32) + b_down.astype(jnp.float32))
    block_output = block_rows.astype(jnp.bfloat16)
    upstream_wide = upstream.astype(jnp.float32)
    grad_w_down = jnp.dot(activated.T, upstream, preferred_element_type=jnp.float32)
    grad_b_down = lax.optimization_barrier(jnp.sum(upstream_wide, axis=0))
    gate_grad = jnp.dot(upstream, w_down.T, preferred_element_type=jnp.float32) * slope
    gate_low = gate_grad.astype(jnp.bfloat16)
    grad_w_up = jnp.dot(second_input.T, gate_low, preferred_element_type=jnp.float32)
    grad_b_up = lax.optimization_barrier(jnp.sum(gate_grad, axis=0))
    grad_second = jnp.dot(gate_low, w_up.T, preferred_element_type=jnp.float32)
    grad_ln2_gain = lax.optimization_barrier(jnp.sum(grad_second * normed_two, axis=0))
    grad_ln2_bias = lax.optimization_barrier(jnp.sum(grad_second, axis=0))
    grad_mid = upstream_wide + norm_backward(grad_second, normed_two, inv_two, ln2_gain.astype(jnp.float32))
    grad_mid_low = grad_mid.astype(jnp.bfloat16)
    grad_w_out = jnp.dot(mixed.T, grad_mid_low, preferred_element_type=jnp.float32)
    grad_b_out = lax.optimization_barrier(jnp.sum(grad_mid, axis=0))
    grad_mixed = jnp.dot(grad_mid_low, w_out.T, preferred_element_type=jnp.float32).astype(jnp.bfloat16)
    grad_heads = split_heads(grad_mixed)
    dprob = jnp.einsum('qhd,khd->hqk', grad_heads, value_heads)
    delta = lax.optimization_barrier(jnp.sum(probs_wide * dprob, axis=-1, keepdims=True))
    dscore = (probs_wide * (dprob - delta) * score_scale).astype(jnp.bfloat16).astype(jnp.float32)
    grad_query = jnp.einsum('hqk,khd->qhd', dscore, key_heads).reshape(seq_len, model_width)
    grad_key = jnp.einsum('hqk,qhd->khd', dscore, query_heads).reshape(seq_len, model_width)
    grad_value = jnp.einsum('hqk,qhd->khd', probs.astype(jnp.float32), grad_heads).reshape(seq_len, model_width)
    grad_proj = jnp.concatenate([grad_query, grad_key, grad_value], axis=1).astype(jnp.bfloat16)
    grad_w_qkv = jnp.dot(first_input.T, grad_proj, preferred_element_type=jnp.float32)
    grad_b_qv = jnp.concatenate([lax.optimization_barrier(jnp.sum(grad_query, axis=0)), lax.optimization_barrier(jnp.sum(grad_value, axis=0))])
    grad_first = jnp.dot(grad_proj, w_qkv.T, preferred_element_type=jnp.float32)
    grad_ln1_gain = lax.optimization_barrier(jnp.sum(grad_first * normed_one, axis=0))
    grad_ln1_bias = lax.optimization_barrier(jnp.sum(grad_first, axis=0))
    grad_input = (grad_mid + norm_backward(grad_first, normed_one, inv_one, ln1_gain.astype(jnp.float32))).astype(jnp.bfloat16)
    grads = (grad_ln1_gain, grad_ln1_bias, grad_w_qkv, grad_b_qv, grad_w_out, grad_b_out, grad_ln2_gain, grad_ln2_bias, grad_w_up, grad_b_up, grad_w_down, grad_b_down)
    return (block_output, grad_input, grads)

def reference(block_input, lengths, ln1_gain, ln1_bias, w_qkv, b_qv, w_out, b_out, ln2_gain, ln2_bias, w_up, b_up, w_down, b_down, cotangent):
    params = (ln1_gain, ln1_bias, w_qkv, b_qv, w_out, b_out, ln2_gain, ln2_bias, w_up, b_up, w_down, b_down)
    starting = tuple((jnp.zeros(param.shape, jnp.float32) for param in params))

    def per_image(totals, item):
        image_in, valid_count, upstream = item
        block_output, grad_input, grads = image_pass(image_in, valid_count, upstream, params)
        return (tuple((total + term for total, term in zip(totals, grads))), (block_output, grad_input))
    totals, stacked = lax.scan(per_image, starting, (block_input, lengths, cotangent))
    return (stacked[0], stacked[1], totals[0], totals[1], totals[2], totals[3], totals[4], totals[5], totals[6], totals[7], totals[8], totals[9], totals[10], totals[11])
```

```python
import functools
import math

import jax
import jax.numpy as jnp
from jax import lax
from jax.experimental import pallas as pl
from jax.experimental.pallas import tpu as pltpu
from jax.sharding import PartitionSpec as P

HEADS = 16
EPSILON = 1e-06
GELU_SCALE = 0.7978845608028654
GELU_CUBIC = 0.044715
NEG_FILL = -1000000000.0

F32 = jnp.float32
BF16 = jnp.bfloat16
QUERY_BLOCK = 256


def layer_norm(values, gain, shift):
    center = values - jnp.mean(values, axis=-1, keepdims=True)
    inv_std = lax.rsqrt(jnp.mean(center * center, axis=-1, keepdims=True) + EPSILON)
    normed = center * inv_std
    return (normed * gain + shift, normed, inv_std)


def norm_backward(upstream, normed, inv_std, gain):
    scaled = upstream * gain
    return inv_std * (
        scaled
        - jnp.mean(scaled, axis=-1, keepdims=True)
        - normed * jnp.mean(scaled * normed, axis=-1, keepdims=True)
    )


def gelu_with_slope(values):
    cubic = values * values * values
    tangent = jnp.tanh(GELU_SCALE * (values + GELU_CUBIC * cubic))
    output = 0.5 * values * (1.0 + tangent)
    slope = 0.5 * (1.0 + tangent) + 0.5 * values * (1.0 - tangent * tangent) * GELU_SCALE * (
        1.0 + 3.0 * GELU_CUBIC * values * values
    )
    return (output, slope)


def hop(values, axis, bit, size):
    return lax.ppermute(values, axis, [(i, i ^ bit) for i in range(size)])


def gather_tokens(block):
    across = hop(block, "grp", 2, 4)
    beside = hop(block, "grp", 1, 4)
    corner = hop(across, "grp", 1, 4)
    return jnp.concatenate([block, beside, across, corner], axis=0)


def scatter_tokens(partial):
    rows = partial.shape[0] // 4
    slots = [partial[s * rows : (s + 1) * rows] for s in range(4)]
    corner = hop(slots[3].astype(BF16), "grp", 1, 4)
    beside = hop(slots[1].astype(BF16), "grp", 1, 4)
    across = hop((slots[2] + corner.astype(F32)).astype(BF16), "grp", 2, 4)
    return slots[0] + beside.astype(F32) + across.astype(F32)


def xor_order(stacked, me):
    return jnp.stack(
        [lax.dynamic_index_in_dim(stacked, jnp.bitwise_xor(me, k), 0, False) for k in range(4)]
    )


def rep_scatter(chunks, rank, count):
    rest = chunks.shape[1:]
    bit = 1
    while bit < count:
        halves = chunks.reshape((chunks.shape[0] // 2, 2) + rest)
        mine = jnp.bitwise_and(rank // bit, 1)
        keep = lax.dynamic_index_in_dim(halves, mine, 1, False)
        give = lax.dynamic_index_in_dim(halves, 1 - mine, 1, False)
        got = hop(give, "rep", bit, count)
        total = keep.astype(F32) + got.astype(F32)
        bit *= 2
        chunks = total if bit >= count else total.astype(BF16)
    return chunks.reshape(rest)


def vector_sum(slots, me, rank_count):
    order = xor_order(slots, me)
    got = hop(order[1::2], "grp", 1, 4)
    pair = order[0::2] + got
    total = pair[0] + hop(pair[1], "grp", 2, 4)
    bit = 1
    while bit < rank_count:
        total = total + hop(total, "rep", bit, rank_count)
        bit *= 2
    return total


def matmul(left, right, contract):
    return lax.dot_general(left, right, ((contract[0], contract[1]), ((), ())),
                           preferred_element_type=F32)


def split_heads(source, target, first, heads, width):
    for head in range(heads):
        start = first + head * width
        target[head, :, 0:width] = source[:, start : start + width]


def attend_forward_kernel(heads, width, proj_ref, live_ref, mixed_ref, total_ref,
                          query, key, value, out):
    rows = proj_ref.shape[0]
    model = heads * width
    for index, target in enumerate((query, key, value)):
        split_heads(proj_ref, target, index * model, heads, width)
    scale = 1.0 / math.sqrt(width)
    blocks = rows // QUERY_BLOCK

    def step(at, carry):
        head = at // blocks
        begin = pl.multiple_of((at % blocks) * QUERY_BLOCK, QUERY_BLOCK)
        q_rows = query[head, pl.ds(begin, QUERY_BLOCK), 0:width]
        k_rows = key[head, :, 0:width]
        v_rows = value[head, :, 0:width]
        scores = matmul(k_rows, q_rows, ((1,), (1,))) * scale
        scores = jnp.where(live_ref[:, 0:1] > 0, scores, NEG_FILL)
        top = jnp.max(scores, axis=0, keepdims=True)
        weights = jnp.exp(scores - top)
        total = jnp.sum(weights, axis=0, keepdims=True)
        probs = (weights * (1.0 / total)).astype(BF16)
        total_ref[head, :, pl.ds(begin, QUERY_BLOCK)] = top + jnp.log(total)
        out[head, pl.ds(begin, QUERY_BLOCK), 0:width] = matmul(
            probs, v_rows, ((0,), (0,))
        ).astype(BF16)
        return carry

    lax.fori_loop(0, heads * blocks, step, 0)
    for head in range(heads):
        mixed_ref[:, head * width : (head + 1) * width] = out[head, :, 0:width]


def attend_forward(proj, live, heads, width):
    rows = proj.shape[0]
    room = pltpu.VMEM((heads, rows, 128), BF16)
    return pl.pallas_call(
        functools.partial(attend_forward_kernel, heads, width),
        out_shape=(
            jax.ShapeDtypeStruct((rows, heads * width), BF16),
            jax.ShapeDtypeStruct((heads, 1, rows), F32),
        ),
        scratch_shapes=[room, room, room, room],
        cost_estimate=pl.CostEstimate(
            flops=4 * heads * rows * rows * 128,
            bytes_accessed=rows * heads * width * 8,
            transcendentals=heads * rows * rows,
        ),
        name="attend_forward",
    )(proj, live)


def attend_backward_kernel(heads, width, proj_ref, live_ref, total_ref, grad_ref,
                           out_ref, sums_ref, query, key, value, grad, dq, dk, dv):
    rows = proj_ref.shape[0]
    model = heads * width
    for index, target in enumerate((query, key, value)):
        split_heads(proj_ref, target, index * model, heads, width)
    split_heads(grad_ref, grad, 0, heads, width)
    dk[...] = jnp.zeros_like(dk)
    dv[...] = jnp.zeros_like(dv)
    scale = 1.0 / math.sqrt(width)
    blocks = rows // QUERY_BLOCK

    def step(at, carry):
        head = at // blocks
        begin = pl.multiple_of((at % blocks) * QUERY_BLOCK, QUERY_BLOCK)
        q_rows = query[head, pl.ds(begin, QUERY_BLOCK), 0:width]
        g_rows = grad[head, pl.ds(begin, QUERY_BLOCK), 0:width]
        k_rows = key[head, :, 0:width]
        v_rows = value[head, :, 0:width]
        scores = matmul(k_rows, q_rows, ((1,), (1,))) * scale
        scores = jnp.where(live_ref[:, 0:1] > 0, scores, NEG_FILL)
        wide = jnp.exp(scores - total_ref[head, :, pl.ds(begin, QUERY_BLOCK)])
        dprob = matmul(v_rows, g_rows, ((1,), (1,)))
        delta = jnp.sum(wide * dprob, axis=0, keepdims=True)
        dscore = (wide * (dprob - delta) * scale).astype(BF16)
        dq[head, pl.ds(begin, QUERY_BLOCK), 0:width] = matmul(dscore, k_rows, ((0,), (0,)))
        dk[head, :, 0:width] += matmul(dscore, q_rows, ((1,), (0,)))
        dv[head, :, 0:width] += matmul(wide.astype(BF16), g_rows, ((1,), (0,)))
        return carry

    lax.fori_loop(0, heads * blocks, step, 0)
    for index, source in enumerate((dq, dk, dv)):
        for head in range(heads):
            start = index * model + head * width
            part = source[head, :, 0:width]
            out_ref[:, start : start + width] = part.astype(BF16)
            sums_ref[0:1, start : start + width] = jnp.sum(part, axis=0, keepdims=True)


def attend_backward(proj, live, log_total, grad_mixed, heads, width):
    rows = proj.shape[0]
    low = pltpu.VMEM((heads, rows, 128), BF16)
    high = pltpu.VMEM((heads, rows, 128), F32)
    return pl.pallas_call(
        functools.partial(attend_backward_kernel, heads, width),
        out_shape=(
            jax.ShapeDtypeStruct((rows, 3 * heads * width), BF16),
            jax.ShapeDtypeStruct((1, 3 * heads * width), F32),
        ),
        scratch_shapes=[low, low, low, low, high, high, high],
        cost_estimate=pl.CostEstimate(
            flops=10 * heads * rows * rows * 128,
            bytes_accessed=rows * heads * width * 14,
            transcendentals=heads * rows * rows,
        ),
        name="attend_backward",
    )(proj, live, log_total, grad_mixed)


def on_device(
    rep_count,
    block_input,
    lengths,
    ln1_gain,
    ln1_bias,
    w_qkv,
    b_qv,
    w_out,
    b_out,
    ln2_gain,
    ln2_bias,
    w_up,
    b_up,
    w_down,
    b_down,
    cotangent,
):
    images, tokens_here, model = block_input.shape
    assert images == 1
    me = lax.axis_index("grp")
    rank = lax.axis_index("rep")
    part = model // 4
    heads = HEADS // 4
    width = model // HEADS

    packed = jnp.concatenate([ln1_gain, ln1_bias, ln2_gain, ln2_bias, b_out, b_down, b_qv])
    packed = xor_order(gather_tokens(packed[None, :]), me).astype(F32)
    names = [packed[:, i * part : (i + 1) * part].reshape(1, model) for i in range(6)]
    gain_one, shift_one, gain_two, shift_two, out_bias, down_bias = names
    qv_bias = packed[:, 6 * part :].reshape(8, part)
    bias_mine = jnp.concatenate(
        [
            lax.dynamic_index_in_dim(qv_bias, me, 0, False),
            jnp.zeros((part,), F32),
            lax.dynamic_index_in_dim(qv_bias, me + 4, 0, False),
        ]
    )

    columns = w_qkv.reshape(part, 3, 4, part).transpose(2, 0, 1, 3).reshape(4, part, 3 * part)
    columns = xor_order(columns, me)
    arrived = jnp.stack([columns[0]] + [hop(columns[s], "grp", s, 4) for s in (1, 2, 3)])
    w_mine = xor_order(arrived, me).reshape(model, 3 * part)

    residual_in = block_input.reshape(tokens_here, model).astype(F32)
    normed_out, normed_one, inv_one = layer_norm(residual_in, gain_one, shift_one)
    first_all = gather_tokens(normed_out.astype(BF16))
    projected = jnp.dot(first_all, w_mine, preferred_element_type=F32) + bias_mine
    proj = projected.astype(BF16)

    slot = jnp.arange(4 * tokens_here, dtype=jnp.int32)
    position = jnp.bitwise_xor(slot // tokens_here, me) * tokens_here + slot % tokens_here
    live = jnp.broadcast_to((position < lengths[0]).astype(F32)[:, None], (4 * tokens_here, 128))
    mixed, log_total = attend_forward(proj, live, heads, width)
    attn = scatter_tokens(jnp.dot(mixed, w_out, preferred_element_type=F32))
    residual_mid = residual_in + (attn + out_bias)

    upstream = cotangent.reshape(tokens_here, model)
    upstream_wide = upstream.astype(F32)
    upstream_all = gather_tokens(upstream)
    back = jnp.einsum("rd,md->rm", upstream_all, w_down, preferred_element_type=F32)

    normed_out2, normed_two, inv_two = layer_norm(residual_mid, gain_two, shift_two)
    second_all = gather_tokens(normed_out2.astype(BF16))
    pre_act = jnp.dot(second_all, w_up, preferred_element_type=F32) + b_up.astype(F32)
    activated_wide, slope = gelu_with_slope(pre_act)
    activated = activated_wide.astype(BF16)
    gate_grad = back * slope
    gate_low = gate_grad.astype(BF16)
    grad_b_up = jnp.sum(gate_grad, axis=0)

    grad_second = scatter_tokens(
        jnp.einsum("rm,dm->rd", gate_low, w_up, preferred_element_type=F32)
    )
    branch = scatter_tokens(jnp.dot(activated, w_down, preferred_element_type=F32))
    block_rows = residual_mid + (branch + down_bias)

    grad_w_up = jnp.einsum("rd,rm->dm", second_all, gate_low, preferred_element_type=F32)
    up_owned = rep_scatter(
        grad_w_up.astype(BF16).reshape(rep_count, model // rep_count, -1), rank, rep_count
    )
    grad_w_down = jnp.einsum("rd,rm->dm", upstream_all, activated, preferred_element_type=F32)
    down_owned = rep_scatter(
        grad_w_down.astype(BF16).reshape(rep_count, model // rep_count, -1), rank, rep_count
    ).T

    grad_mid = upstream_wide + norm_backward(grad_second, normed_two, inv_two, gain_two)
    mid_all = gather_tokens(grad_mid.astype(BF16))
    grad_mixed = jnp.einsum("rd,ed->re", mid_all, w_out, preferred_element_type=F32).astype(BF16)
    grad_w_out = jnp.einsum("rd,re->de", mid_all, mixed, preferred_element_type=F32)
    out_owned = rep_scatter(
        grad_w_out.astype(BF16).reshape(rep_count, model // rep_count, -1), rank, rep_count
    ).T

    hidden = b_up.shape[0]
    feature_sums = jnp.stack(
        [
            jnp.sum(grad_second * normed_two, axis=0),
            jnp.sum(grad_second, axis=0),
            jnp.sum(grad_mid, axis=0),
            jnp.sum(upstream_wide, axis=0),
        ]
    )
    feature_slots = feature_sums.reshape(4, 4, part).transpose(1, 0, 2).reshape(4, 4 * part)
    is_me = (jnp.arange(4) == me)[:, None]
    early = vector_sum(
        jnp.concatenate([feature_slots, jnp.where(is_me, grad_b_up[None, :], 0.0)], axis=1),
        me,
        rep_count,
    )

    grad_proj, proj_sums = attend_backward(proj, live, log_total, grad_mixed, heads, width)
    grad_first = scatter_tokens(
        jnp.einsum("rc,dc->rd", grad_proj, w_mine, preferred_element_type=F32)
    )
    qkv_terms = jnp.einsum("rd,rc->dc", first_all, grad_proj, preferred_element_type=F32)
    qkv_terms = xor_order(qkv_terms.astype(BF16).reshape(4, part, 3 * part), me)
    arrived = jnp.stack([qkv_terms[0]] + [hop(qkv_terms[s], "grp", s, 4) for s in (1, 2, 3)])
    arrived = xor_order(arrived, me)
    arrived = arrived.reshape(4, part, 3, part).transpose(1, 2, 0, 3)
    arrived = arrived.reshape(part, rep_count, 3 * model // rep_count).transpose(1, 0, 2)
    qkv_owned = rep_scatter(arrived, rank, rep_count)

    gain_one_term = jnp.sum(grad_first * normed_one, axis=0)
    shift_one_term = jnp.sum(grad_first, axis=0)
    grad_rows = grad_mid + norm_backward(grad_first, normed_one, inv_one, gain_one)

    eighth = jnp.arange(8)[:, None]
    query_slot = jnp.where(eighth == me, proj_sums[:, :part], 0.0)
    value_slot = jnp.where(eighth == me + 4, proj_sums[:, 2 * part :], 0.0)
    late = vector_sum(
        jnp.concatenate(
            [
                gain_one_term.reshape(4, part),
                shift_one_term.reshape(4, part),
                (query_slot + value_slot).reshape(4, 2 * part),
            ],
            axis=1,
        ),
        me,
        rep_count,
    )

    image_shape = (images, tokens_here, model)
    return (
        block_rows.astype(BF16).reshape(image_shape),
        grad_rows.astype(BF16).reshape(image_shape),
        late[:part],
        late[part : 2 * part],
        qkv_owned,
        late[2 * part :],
        out_owned,
        early[2 * part : 3 * part],
        early[:part],
        early[part : 2 * part],
        up_owned,
        early[4 * part :],
        down_owned,
        early[3 * part : 4 * part],
    )


def solution(mesh):
    in_specs = (
        P("rep", "grp", None),
        P("rep"),
        P("grp"),
        P("grp"),
        P("grp", None),
        P("grp"),
        P("grp", None),
        P("grp"),
        P("grp"),
        P("grp"),
        P(None, "grp"),
        P("grp"),
        P("grp", None),
        P("grp"),
        P("rep", "grp", None),
    )
    out_specs = (
        P("rep", "grp", None),
        P("rep", "grp", None),
        P("grp"),
        P("grp"),
        P("grp", "rep"),
        P("grp"),
        P("grp", "rep"),
        P("grp"),
        P("grp"),
        P("grp"),
        P("rep", "grp"),
        P("grp"),
        P("grp", "rep"),
        P("grp"),
    )
    return jax.shard_map(
        functools.partial(on_device, mesh.shape["rep"]),
        mesh=mesh,
        in_specs=in_specs,
        out_specs=out_specs,
        check_vma=False,
    )
```
